256 devices in a mesh: ctx: 16 (over y_lo, x, core), chan: 16 (over z, y_hi).
Axes of the slice: x: 4, y: 4 (y_hi: 2, y_lo: 2; y = y_hi * 2 + y_lo), z: 8, core: 2. Of those that a mesh axis runs over, the one named last changes fastest.
Arguments:
- features: bfloat16 [3, 4096, 4096], P(None, 'ctx', 'chan'), may hold values from -6 to 6
- saved_conv: bfloat16 [4096, 4096], P('ctx', 'chan'), may hold values from -6 to 6
- grad_out: bfloat16 [4096, 4096], P('ctx', 'chan'), may hold values from -6 to 6
- out_weight: bfloat16 [4096, 4096], P('chan'), may hold values from -0.09375 to 0.09375
- in_weight: bfloat16 [3, 4096, 4096], P(None, None, 'chan'), may hold values from -0.09375 to 0.09375
- short_taps: float32 [3, 3, 4096], P(None, None, 'chan'), may hold values from -3.5 to 3.5
- residues: float32 [16, 4096], P(None, 'chan'), may hold values from -1 to 1
- decay_time: float32 [16, 4096], P(None, 'chan'), may hold values from 25 to 20480
Outputs:
- grad_input: bfloat16 [4096, 4096], P('chan', 'ctx')
- grad_residue: float32 [16, 4096], P(None, 'chan')
The draws below stay inside these ranges and needn't reach their ends.
All inputs are finite; a program needn't handle non-finite values.
Results may differ from the reference program's by a relative error of at most 0.019.
Values may be sent and summed in bfloat16 or wider, within the bound.
A program may use at most 64 MiB of HBM per device.

```python
import jax
import jax.numpy as jnp
from jax import lax

D = 4096
MODES = 16
TAPS = 3
TOKENS = 4096
N_CHAN = 16


def draw_residues(key, part):
    scale = (8.0 * TOKENS) ** (-0.5)
    values = jnp.clip(jax.random.normal(key, (MODES, D), jnp.float32), -6.0, 6.0) * scale
    return values.astype(jnp.float32)


def draw_decay_time(key, part):
    first, second, third = jax.random.split(key, 3)
    share = 0.5
    slow_low = jnp.log(0.5 * TOKENS)
    slow = jnp.exp(jax.random.uniform(first, (MODES, D), jnp.float32, slow_low, jnp.log(5.0 * TOKENS)))
    fast = jnp.exp(jax.random.uniform(second, (MODES, D), jnp.float32, jnp.log(25.0), jnp.log(50.0)))
    pick = jax.random.bernoulli(third, share, (MODES, D))
    return jnp.where(pick, slow, fast).astype(jnp.float32)


def level_of(stream_key, dims, pieces, smallest, high):
    gain = 1.0
    for dim, shards_of in pieces:
        steps = jax.random.uniform(jax.random.fold_in(jax.random.fold_in(stream_key, 6), dim), (shards_of,), jnp.float32, smallest / len(pieces), high / len(pieces))
        gain = gain * jnp.repeat(jnp.exp(steps), dims[dim] // shards_of).reshape((-1,) + (1,) * (len(dims) - 1 - dim))
    return gain


def gaussian(stream_key, dims, width, reach, shards=(), held_as=jnp.bfloat16):
    factor_of = level_of(stream_key, dims, shards, -0.22, 0.18) if shards else 1.0
    values = jax.random.normal(stream_key, dims, jnp.float32) * width * factor_of
    return jnp.minimum(jnp.maximum(values, -reach), reach).astype(held_as)


def setup_inputs(seed: int = 0) -> dict:
    key_list = jax.random.split(jax.random.key(seed), 9)
    features = gaussian(key_list[0], (3, TOKENS, D), 1.0, 6.0, ((1, 16), (2, 16)))
    saved_conv = gaussian(key_list[1], (TOKENS, D), 1.0, 6.0, ((0, 16), (1, 16)))
    grad_out = gaussian(key_list[2], (TOKENS, D), 1.0, 6.0, ((0, 16), (1, 16)))
    out_weight = gaussian(key_list[3], (D, D), D ** -0.5, 0.09375, ((0, 16),))
    in_weight = gaussian(key_list[4], (3, D, D), D ** -0.5, 0.09375, ((2, 16),))
    short_taps = gaussian(key_list[5], (3, TAPS, D), TAPS ** -0.5, 3.5, ((2, 16),), jnp.float32)
    residues = draw_residues(jax.random.fold_in(key_list[8], 71), 0)
    decay_time = draw_decay_time(jax.random.fold_in(key_list[8], 71), 0)
    return {"features": features, "saved_conv": saved_conv, "grad_out": grad_out, "out_weight": out_weight, "in_weight": in_weight, "short_taps": short_taps, "residues": residues, "decay_time": decay_time}


def reference(features, saved_conv, grad_out, out_weight, in_weight, short_taps, residues, decay_time):
    highest = lax.Precision.HIGHEST
    acts = features.astype(jnp.float32)
    query_act = acts[0]
    key_act = acts[1]
    value_act = acts[2]
    grad_gate = jnp.dot(grad_out.astype(jnp.float32), out_weight.astype(jnp.float32).T, precision=highest)
    grad_conv = grad_gate * query_act
    grad_query = grad_gate * saved_conv.astype(jnp.float32)
    product = key_act * value_act
    decay = jnp.exp(-1.0 / decay_time)

    def advance(carry, inputs):
        state, total = carry
        grad_row, prod_row = inputs
        state = grad_row[None, :] + decay * state
        total = total + prod_row[None, :] * state
        return (state, total), jnp.sum(residues * state, axis=0)

    start = (jnp.zeros(residues.shape, jnp.float32), jnp.zeros(residues.shape, jnp.float32))
    (state, total), grad_product = lax.scan(advance, start, (grad_conv, product), reverse=True)
    grad_key = grad_product * value_act
    grad_value = grad_product * key_act
    grad_acts = jnp.stack([grad_query, grad_key, grad_value])
    padded = jnp.pad(grad_acts, ((0, 0), (0, TAPS - 1), (0, 0)))
    filtered = short_taps[:, 0, None, :] * padded[:, 0:TOKENS, :]
    for lag in range(1, TAPS):
        filtered = filtered + short_taps[:, lag, None, :] * padded[:, lag:lag + TOKENS, :]
    grad_proj = filtered.astype(jnp.bfloat16)
    group_width = D // N_CHAN
    accum = jnp.zeros((D, TOKENS), jnp.float32)
    for group in range(N_CHAN):
        low = group * group_width
        high = low + group_width
        term = jnp.zeros((D, TOKENS), jnp.float32)
        for which in range(3):
            term = term + jnp.dot(in_weight[which][:, low:high].astype(jnp.float32), grad_proj[which][:, low:high].astype(jnp.float32).T, precision=highest)
        rounded = lax.optimization_barrier(term.astype(jnp.bfloat16))
        accum = accum + rounded.astype(jnp.float32)
    return accum.astype(jnp.bfloat16), total / TOKENS
```

```python
import functools

import jax
import jax.numpy as jnp
from jax import lax
from jax.experimental import pallas as pl
from jax.experimental.pallas import tpu as pltpu
from jax.sharding import PartitionSpec as P

MESH = pl.DeviceIdType.MESH
F32 = jnp.float32
BF16 = jnp.bfloat16
NT = (((1,), (1,)), ((), ()))
CHAINS = 4


def kernel(
    go, feat, conv, ow, iw, taps, res, decay,
    out, gres,
    blocks, owv, iwv, fv, cv, tv, rv, dv,
    acc, grow, prod, acts, gp, gprod, lam_ref, ent, csum,
    sown, sin, hsend, hrecv, kvh, rown, rin,
    part, tx, rx, ysend, yrecv,
    in_sem, ag_s, ag_r, agy_s, agy_r, kv_s, kv_r, h_s, h_r,
    s_s, s_r, r_s, r_r, rs_s, rs_r, rsy_s, rsy_r,
):
    n_ctx = lax.axis_size("ctx")
    n_z = lax.axis_size("chan") // 2
    me = lax.axis_index("ctx")
    ch = lax.axis_index("chan")
    z = ch // 2
    yh = lax.rem(ch, 2)
    length = acc.shape[0]
    half_rows = length // 2

    def chan_of(zz, yy):
        return lax.rem(zz + 2 * n_z, n_z) * 2 + yy

    partner = chan_of(z, 1 - yh)
    sides = [chan_of(z + 1, yh), chan_of(z - 1, yh)]
    dirs = (1, -1)

    pairs = [(go, blocks.at[ch]), (ow, owv), (feat, fv), (conv, cv), (taps, tv),
             (res, rv), (decay, dv), (iw, iwv)]
    local = [pltpu.make_async_copy(a, b, in_sem.at[i]) for i, (a, b) in enumerate(pairs)]
    for c in local:
        c.start()

    barrier = pltpu.get_barrier_semaphore()
    for dst in (sides[0], sides[1], partner):
        pl.semaphore_signal(barrier, inc=1, device_id={"chan": dst}, device_id_type=MESH)
    for k in range(1, n_ctx):
        pl.semaphore_signal(
            barrier, inc=1, device_id={"ctx": lax.rem(me + k, n_ctx)}, device_id_type=MESH
        )
    pl.semaphore_wait(barrier, 3 + n_ctx - 1)

    def remote(src, dst, ss, rs, **where):
        return pltpu.make_async_remote_copy(
            src_ref=src, dst_ref=dst, send_sem=ss, recv_sem=rs,
            device_id=where, device_id_type=MESH,
        )

    def rows(half):
        return pl.ds(half * half_rows, half_rows)

    def ag(d, q, h, half, receiving=False):
        slot = (2 * h + half) if h < 3 else 6
        source = z - dirs[d] * (h + (1 if receiving else 0))
        block = chan_of(source, yh if q == 0 else 1 - yh)
        ref = blocks.at[block, rows(half)]
        src = go.at[rows(half)] if (q == 0 and h == 0 and not receiving) else ref
        return remote(src, ref, ag_s.at[d, q, slot], ag_r.at[d, q, slot], chan=sides[d])

    def agy(half, receiving=False):
        ref = blocks.at[partner if receiving else ch, rows(half)]
        src = ref if receiving else go.at[rows(half)]
        return remote(src, ref, agy_s.at[half], agy_r.at[half], chan=partner)

    sent = []

    def send(c):
        c.start()
        sent.append(c)

    for half in range(2):
        for d in range(2):
            send(ag(d, 0, 0, half))
        send(agy(half))

    prev = lax.rem(me + n_ctx - 1, n_ctx)

    @pl.when(me > 0)
    def _():
        remote(feat.at[pl.ds(1, 2), pl.ds(0, 16)], kvh, kv_s.at[0], kv_r.at[0], ctx=prev).start()

    @pl.when(me == n_ctx - 1)
    def _():
        kvh[...] = jnp.zeros_like(kvh)
        hrecv[...] = jnp.zeros_like(hrecv)

    first = [True]

    def multiply(block):
        cols = pl.ds(pl.multiple_of(block * length, length), length)
        term = lax.dot_general(blocks[block], owv[:, cols], NT, preferred_element_type=F32)
        if first[0]:
            acc[...] = term
            first[0] = False
        else:
            acc[...] += term

    local[0].wait()
    local[1].wait()
    multiply(ch)
    for q in range(2):
        other = yh if q == 0 else 1 - yh
        if q == 1:
            for half in range(2):
                agy(half, True).wait_recv()
                for d in range(2):
                    send(ag(d, 1, 0, half))
            multiply(partner)
        for h in range(1, 4):
            for half in range(2):
                for d in range(2):
                    ag(d, q, h - 1, half, True).wait_recv()
                    if h < 3 or half == d:
                        send(ag(d, q, h, half))
            multiply(chan_of(z - h, other))
            multiply(chan_of(z + h, other))
        if q == 0:
            for i in range(2, 7):
                local[i].wait()
            rate = 1.0 / dv[...]
            lam_ref[0] = jnp.exp(-rate)
            lam_ref[1] = jnp.exp(-rate * (length // CHAINS))
            lam_ref[2] = jnp.exp(-rate * length)
            lam_ref[3] = jnp.exp(rate)
            prod[...] = fv[1].astype(F32) * fv[2].astype(F32)
        for d in range(2):
            ag(d, q, 3, d, True).wait_recv()
        multiply(chan_of(z + n_z // 2, other))

    gate = acc[...]
    grow[...] = gate * fv[0].astype(F32)
    acts[0, pl.ds(0, length)] = gate * cv[...].astype(F32)

    @pl.when(me > 0)
    def _():
        hsend[pl.ds(0, 8)] = acts[0, pl.ds(0, 8)]
        hsend[pl.ds(8, 8)] = grow[pl.ds(0, 8)]
        remote(hsend, hrecv, h_s.at[0], h_r.at[0], ctx=prev).start()

    run = length // CHAINS
    lam = lam_ref[0]

    def sum_step(i, carry):
        fresh = []
        for k in range(CHAINS):
            g = grow[pl.ds(k * run + run - 1 - i, 1)]
            fresh.append(g + lam * carry[k])
        return tuple(fresh)

    zero = jnp.zeros_like(lam)
    sums = lax.fori_loop(0, run, sum_step, (zero,) * CHAINS, unroll=8)
    total = sums[CHAINS - 1]
    for k in range(CHAINS - 2, -1, -1):
        total = sums[k] + lam_ref[1] * total
    for k in range(CHAINS):
        csum[k] = sums[k]
    sown[...] = total

    for k in range(1, n_ctx):
        @pl.when(me >= k)
        def _():
            dst = lax.rem(me + n_ctx - k, n_ctx)
            remote(sown, sin.at[me], s_s.at[k], s_r.at[me], ctx=dst).start()

    @pl.when(me < n_ctx - 1)
    def _():
        nxt = lax.rem(me + 1, n_ctx)
        remote(hsend, hrecv, h_s.at[0], h_r.at[0], ctx=nxt).wait_recv()
        remote(feat.at[pl.ds(1, 2), pl.ds(0, 16)], kvh, kv_s.at[0], kv_r.at[0], ctx=nxt).wait_recv()

    acts[0, pl.ds(length, 8)] = hrecv[pl.ds(0, 8)]

    def short(i):
        y = tv[i, pl.ds(0, 1)] * acts[i, pl.ds(0, length)]
        y = y + tv[i, pl.ds(1, 1)] * acts[i, pl.ds(1, length)]
        y = y + tv[i, pl.ds(2, 1)] * acts[i, pl.ds(2, length)]
        gp[i] = y.astype(BF16)

    short(0)

    ent[...] = jnp.zeros_like(ent)
    for j in range(n_ctx - 1, 0, -1):
        @pl.when(j > me)
        def _():
            remote(sown, sin.at[j], s_s.at[0], s_r.at[j], ctx=j).wait_recv()
            ent[...] = sin[j] + lam_ref[2] * ent[...]

    entering = ent[...]
    residue = rv[...]
    starts = [None] * CHAINS
    starts[CHAINS - 1] = entering
    for k in range(CHAINS - 2, -1, -1):
        starts[k] = csum[k + 1] + lam_ref[1] * starts[k + 1]

    def full_step(i, carry):
        states, totals = carry
        fresh, summed = [], []
        for k in range(CHAINS):
            r = k * run + run - 1 - i
            s = grow[pl.ds(r, 1)] + lam * states[k]
            gprod[pl.ds(r, 1)] = jnp.sum(residue * s, axis=0, keepdims=True)
            totals = totals + prod[pl.ds(r, 1)] * s
            fresh.append(s)
        return tuple(fresh), totals

    _, totals = lax.fori_loop(0, run, full_step, (tuple(starts), zero), unroll=4)
    rown[...] = totals
    beyond = (entering - hrecv[pl.ds(8, 1)]) * lam_ref[3]
    gprod[pl.ds(length, 1)] = jnp.sum(residue * entering, axis=0, keepdims=True)
    gprod[pl.ds(length + 1, 1)] = jnp.sum(residue * beyond, axis=0, keepdims=True)
    acts[1, pl.ds(0, length)] = gprod[pl.ds(0, length)] * fv[2].astype(F32)
    acts[2, pl.ds(0, length)] = gprod[pl.ds(0, length)] * fv[1].astype(F32)
    acts[1, pl.ds(length, 2)] = gprod[pl.ds(length, 2)] * kvh[1, pl.ds(0, 2)].astype(F32)
    acts[2, pl.ds(length, 2)] = gprod[pl.ds(length, 2)] * kvh[0, pl.ds(0, 2)].astype(F32)
    short(1)
    short(2)

    local[7].wait()

    def own_part(dest):
        at = pl.ds(pl.multiple_of(dest * length, length), length)
        y = lax.dot_general(iwv[0, at], gp[0], NT, preferred_element_type=F32)
        y = y + lax.dot_general(iwv[1, at], gp[1], NT, preferred_element_type=F32)
        y = y + lax.dot_general(iwv[2, at], gp[2], NT, preferred_element_type=F32)
        part[dest] = y

    def rs(d, q, slot):
        return remote(tx.at[d, q, slot], rx.at[d, q, slot], rs_s.at[d, q, slot],
                      rs_r.at[d, q, slot], chan=sides[d])

    def rs_send(d, q, slot, dest, half, before):
        y = part[dest, rows(half)]
        if before is not None:
            rs(d, q, before).wait_recv()
            y = y + rx[d, q, before].astype(F32)
        tx[d, q, slot] = y.astype(BF16)
        send(rs(d, q, slot))

    def residue_sends():
        for k in range(1, n_ctx):
            dst = lax.rem(me + n_ctx - k, n_ctx)
            send(remote(rown, rin.at[me], r_s.at[k], r_r.at[me], ctx=dst))

    def ycopy(half):
        return remote(ysend.at[half], yrecv.at[half], rsy_s.at[half], rsy_r.at[half], chan=partner)

    for q in range(2):
        owner = 1 - yh if q == 0 else yh
        far = chan_of(z + 4, owner)
        own_part(far)
        for d in range(2):
            rs_send(d, q, 0, far, d, None)
        near = {}
        for h in (3, 2, 1):
            for d in range(2):
                near[d, h] = chan_of(z + dirs[d] * h, owner)
                own_part(near[d, h])
            for late in range(2):
                for d in range(2):
                    half = d if late else 1 - d
                    slot = 1 + 2 * (3 - h) + late
                    if h == 3:
                        before = 0 if late else None
                    else:
                        before = slot - 2
                    rs_send(d, q, slot, near[d, h], half, before)
            if q == 0 and h == 3:
                residue_sends()
        mine = chan_of(z, owner)
        own_part(mine)
        for late in range(2):
            for d in range(2):
                rs(d, q, 5 + late).wait_recv()
        for half in range(2):
            y = part[mine, rows(half)]
            y = y + rx[0, q, 6 if half == 0 else 5].astype(F32)
            y = y + rx[1, q, 5 if half == 0 else 6].astype(F32)
            if q == 0:
                ysend[half] = y.astype(BF16)
                send(ycopy(half))
            else:
                ycopy(half).wait_recv()
                out[rows(half)] = (y + yrecv[half].astype(F32)).astype(BF16)

    rin[me] = rown[...]
    for k in range(1, n_ctx):
        src = lax.rem(me + k, n_ctx)
        remote(rown, rin.at[src], r_s.at[0], r_r.at[src], ctx=src).wait_recv()
    y = rin[0]
    for j in range(1, n_ctx):
        y = y + rin[j]
    gres[...] = y / (length * n_ctx)

    for c in sent:
        c.wait_send()
    for k in range(1, n_ctx):
        @pl.when(me >= k)
        def _():
            dst = lax.rem(me + n_ctx - k, n_ctx)
            remote(sown, sin.at[me], s_s.at[k], s_r.at[me], ctx=dst).wait_send()

    @pl.when(me > 0)
    def _():
        remote(hsend, hrecv, h_s.at[0], h_r.at[0], ctx=prev).wait_send()
        remote(feat.at[pl.ds(1, 2), pl.ds(0, 16)], kvh, kv_s.at[0], kv_r.at[0], ctx=prev).wait_send()


def local(features, saved_conv, grad_out, out_weight, in_weight, short_taps, residues, decay_time):
    length, width = grad_out.shape
    modes = residues.shape[0]
    n_chan = lax.axis_size("chan")
    n_ctx = lax.axis_size("ctx")
    half = length // 2
    dma = pltpu.SemaphoreType.DMA
    any_spec = pl.BlockSpec(memory_space=pl.ANY)
    vmem = pl.BlockSpec(memory_space=pltpu.VMEM)
    scratch = [
        pltpu.VMEM((n_chan, length, width), BF16),
        pltpu.VMEM(out_weight.shape, BF16),
        pltpu.VMEM(in_weight.shape, BF16),
        pltpu.VMEM(features.shape, BF16),
        pltpu.VMEM((length, width), BF16),
        pltpu.VMEM(short_taps.shape, F32),
        pltpu.VMEM((modes, width), F32),
        pltpu.VMEM((modes, width), F32),
        pltpu.VMEM((length, width), F32),
        pltpu.VMEM((length, width), F32),
        pltpu.VMEM((length, width), F32),
        pltpu.VMEM((3, length + 8, width), F32),
        pltpu.VMEM((3, length, width), BF16),
        pltpu.VMEM((length + 8, width), F32),
        pltpu.VMEM((4, modes, width), F32),
        pltpu.VMEM((modes, width), F32),
        pltpu.VMEM((CHAINS, modes, width), F32),
        pltpu.VMEM((modes, width), F32),
        pltpu.VMEM((n_ctx, modes, width), F32),
        pltpu.VMEM((16, width), F32),
        pltpu.VMEM((16, width), F32),
        pltpu.VMEM((2, 16, width), BF16),
        pltpu.VMEM((modes, width), F32),
        pltpu.VMEM((n_ctx, modes, width), F32),
        pltpu.VMEM((n_chan, length, width), F32),
        pltpu.VMEM((2, 2, 7, half, width), BF16),
        pltpu.VMEM((2, 2, 7, half, width), BF16),
        pltpu.VMEM((2, half, width), BF16),
        pltpu.VMEM((2, half, width), BF16),
        dma((8,)), dma((2, 2, 7)), dma((2, 2, 7)), dma((2,)), dma((2,)),
        dma((1,)), dma((1,)), dma((1,)), dma((1,)),
        dma((n_ctx,)), dma((n_ctx,)), dma((n_ctx,)), dma((n_ctx,)),
        dma((2, 2, 7)), dma((2, 2, 7)), dma((2,)), dma((2,)),
    ]
    return pl.pallas_call(
        kernel,
        out_shape=(
            jax.ShapeDtypeStruct((length, width), BF16),
            jax.ShapeDtypeStruct((modes, width), F32),
        ),
        in_specs=[any_spec] * 8,
        out_specs=(vmem, vmem),
        scratch_shapes=scratch,
        compiler_params=pltpu.CompilerParams(
            collective_id=0, has_side_effects=True, vmem_limit_bytes=48 * 1024 * 1024
        ),
    )(grad_out, features, saved_conv, out_weight, in_weight, short_taps, residues, decay_time)


def solution(mesh):
    return jax.shard_map(
        local,
        mesh=mesh,
        in_specs=(
            P(None, "ctx", "chan"),
            P("ctx", "chan"),
            P("ctx", "chan"),
            P("chan", None),
            P(None, None, "chan"),
            P(None, None, "chan"),
            P(None, "chan"),
            P(None, "chan"),
        ),
        out_specs=(P("chan", "ctx"), P(None, "chan")),
        check_vma=False,
    )
```

```python
import functools

import jax
import jax.numpy as jnp
from jax import lax
from jax.experimental import pallas as pl
from jax.experimental.pallas import tpu as pltpu
from jax.sharding import PartitionSpec as P

MESH = pl.DeviceIdType.MESH
F32 = jnp.float32
BF16 = jnp.bfloat16
NT = (((1,), (1,)), ((), ()))
CHAINS = 4

PIECES = 2
WIRE, HOP_Z, HOP_Y, AHEAD = 3.08 / PIECES, 1.7, 2.5, 1.6
CROSS = {1: (0, 1), 2: (), 3: (0, 1), 4: ()}
OFFSETS = (-3, -2, -1, 0, 1, 2, 3, 4)


def origin(item, link):
    plane, off, piece = item
    if link == "y":
        return (0, off, piece)
    if link == "+":
        return (plane, (off if off < 4 else -4) + 1, piece)
    return (plane, off - 1, piece)


def schedule():
    link = {}
    for plane in (0, 1):
        for off in OFFSETS:
            for piece in range(PIECES):
                if off == 0:
                    how = "y" if plane else "own"
                elif plane and piece in CROSS[abs(off)]:
                    how = "y"
                elif off == 4:
                    how = "+" if piece < PIECES // 2 else "-"
                else:
                    how = "+" if off < 0 else "-"
                link[plane, off, piece] = how
    kids = {item: [] for item in link}
    for item, how in link.items():
        if how != "own":
            kids[origin(item, how)].append(item)

    def hop(item):
        return HOP_Y if link[item] == "y" else HOP_Z

    def height(item):
        return max([WIRE + hop(k) + height(k) for k in kids[item]], default=0.0)

    free = {"+": 0.0, "-": 0.0, "y": 0.0}
    queue = {"+": [], "-": [], "y": []}
    pending = [(0.0, p, (0, 0, p)) for p in range(PIECES)]
    here, start, now, count = {}, {}, 0.0, PIECES
    while True:
        times = [p[0] for p in pending] + [max(free[c], now) for c in queue if queue[c]]
        if not times:
            break
        now = min(times)
        for entry in sorted(p for p in pending if p[0] <= now + 1e-9):
            pending.remove(entry)
            here[entry[2]] = entry[0]
            for k in kids[entry[2]]:
                queue[link[k]].append((-height(k), now, k))
        for c in queue:
            if queue[c] and free[c] <= now + 1e-9:
                queue[c].sort()
                k = queue[c].pop(0)[2]
                start[k], free[c] = now, now + WIRE
                pending.append((now + WIRE + hop(k), count, k))
                count += 1
    return link, kids, here, start


LINK, KIDS, HERE, START = schedule()
ITEMS = sorted(START)
INDEX = {item: i for i, item in enumerate(ITEMS)}
END = max(HERE.values())


def kernel(
    go, feat, conv, ow, iw, taps, res, decay,
    out, gres,
    blocks, owv, iwv, fv, cv, tv, rv, dv,
    acc, grow, prod, acts, gp, gprod, lam_ref, ent, csum,
    sown, sin, hsend, hrecv, kvh, rown, rin,
    part, tx, rx,
    in_sem, ag_s, ag_r, kv_s, kv_r, h_s, h_r,
    s_s, s_r, r_s, r_r, rs_s, rs_r,
):
    n_ctx = lax.axis_size("ctx")
    n_z = lax.axis_size("chan") // 2
    me = lax.axis_index("ctx")
    ch = lax.axis_index("chan")
    z = ch // 2
    yh = lax.rem(ch, 2)
    length = acc.shape[0]

    def chan_of(zz, yy):
        return lax.rem(zz + 2 * n_z, n_z) * 2 + yy

    partner = chan_of(z, 1 - yh)
    sides = [chan_of(z + 1, yh), chan_of(z - 1, yh)]

    pairs = [(go, blocks.at[ch]), (ow, owv), (feat, fv), (conv, cv), (taps, tv),
             (res, rv), (decay, dv), (iw, iwv)]
    local = [pltpu.make_async_copy(a, b, in_sem.at[i]) for i, (a, b) in enumerate(pairs)]
    for c in local:
        c.start()
    seen = set()

    def ready(*which):
        for i in which:
            if i not in seen:
                local[i].wait()
                seen.add(i)
    seen = set()

    def ready(*which):
        for i in which:
            if i not in seen:
                local[i].wait()
                seen.add(i)

    barrier = pltpu.get_barrier_semaphore()
    for dst in (sides[0], sides[1], partner):
        pl.semaphore_signal(barrier, inc=1, device_id={"chan": dst}, device_id_type=MESH)
    for k in range(1, n_ctx):
        pl.semaphore_signal(
            barrier, inc=1, device_id={"ctx": lax.rem(me + k, n_ctx)}, device_id_type=MESH
        )
    pl.semaphore_wait(barrier, 3 + n_ctx - 1)

    def remote(src, dst, ss, rs, **where):
        return pltpu.make_async_remote_copy(
            src_ref=src, dst_ref=dst, send_sem=ss, recv_sem=rs,
            device_id=where, device_id_type=MESH,
        )

    piece_rows = length // PIECES

    def rows(piece):
        return pl.ds(piece * piece_rows, piece_rows)

    def place(item):
        return chan_of(z + item[1], yh if item[0] == 0 else 1 - yh)

    onward = {"+": sides[0], "-": sides[1], "y": partner}
    back = {"+": sides[1], "-": sides[0], "y": partner}

    def ag(item, receiving=False):
        held = item if receiving else origin(item, LINK[item])
        ref = blocks.at[place(held), rows(item[2])]
        src = go.at[rows(item[2])] if LINK[held] == "own" else ref
        i = INDEX[item]
        return remote(src, ref, ag_s.at[i], ag_r.at[i], chan=onward[LINK[item]])

    sent = []
    guarded = []

    def finish():
        for c in sent:
            c.wait_send()
        for cond, c in guarded:
            pl.when(cond)(c.wait_send)

    def send_if(cond, c):
        pl.when(cond)(c.start)
        guarded.append((cond, c))

    def send(c):
        c.start()
        sent.append(c)

    steps = []
    for item in ITEMS:
        steps.append((max(HERE[origin(item, LINK[item])], START[item] - AHEAD), 1, item))
        steps.append((HERE[item], 0, item))
    steps.sort(key=lambda step: (step[0], step[1], START[step[2]]))
    head = [step for step in steps if step[1] == 1 and step[0] == 0.0]
    for _, _, item in head:
        send(ag(item))

    prev = lax.rem(me + n_ctx - 1, n_ctx)

    send_if(me > 0, remote(feat.at[pl.ds(1, 2), pl.ds(0, 16)], kvh, kv_s.at[0], kv_r.at[0], ctx=prev))

    @pl.when(me == n_ctx - 1)
    def _():
        kvh[...] = jnp.zeros_like(kvh)
        hrecv[...] = jnp.zeros_like(hrecv)

    first = [True]

    def multiply(block):
        cols = pl.ds(pl.multiple_of(block * length, length), length)
        term = lax.dot_general(blocks[block], owv[:, cols], NT, preferred_element_type=F32)
        if first[0]:
            acc[...] = term
            first[0] = False
        else:
            acc[...] += term

    ready(0, 1)
    multiply(ch)
    waiting = []
    arrived = {}
    prepared = False
    for when, kind, item in steps[len(head):]:
        if kind == 1:
            send(ag(item))
            continue
        ag(item, True).wait_recv()
        arrived[item[:2]] = arrived.get(item[:2], 0) + 1
        if waiting:
            multiply(place(waiting.pop(0) + (0,)))
        if arrived[item[:2]] == PIECES:
            waiting.append(item[:2])
        if not prepared and len(arrived) > 2:
            prepared = True
            ready(2, 3, 4, 5, 6)
            rate = 1.0 / dv[...]
            lam_ref[0] = jnp.exp(-rate)
            lam_ref[1] = jnp.exp(-rate * (length // CHAINS))
            lam_ref[2] = jnp.exp(-rate * length)
            lam_ref[3] = jnp.exp(rate)
            prod[...] = fv[1].astype(F32) * fv[2].astype(F32)
    for block in waiting:
        multiply(place(block + (0,)))

    gate = acc[...]
    grow[...] = gate * fv[0].astype(F32)
    acts[0, pl.ds(0, length)] = gate * cv[...].astype(F32)

    @pl.when(me > 0)
    def _():
        hsend[pl.ds(0, 8)] = acts[0, pl.ds(0, 8)]
        hsend[pl.ds(8, 8)] = grow[pl.ds(0, 8)]

    send_if(me > 0, remote(hsend, hrecv, h_s.at[0], h_r.at[0], ctx=prev))

    run = length // CHAINS
    lam = lam_ref[0]

    def sum_step(i, carry):
        fresh = []
        for k in range(CHAINS):
            g = grow[pl.ds(k * run + run - 1 - i, 1)]
            fresh.append(g + lam * carry[k])
        return tuple(fresh)

    zero = jnp.zeros_like(lam)
    sums = lax.fori_loop(0, run, sum_step, (zero,) * CHAINS, unroll=8)
    total = sums[CHAINS - 1]
    for k in range(CHAINS - 2, -1, -1):
        total = sums[k] + lam_ref[1] * total
    for k in range(CHAINS):
        csum[k] = sums[k]
    sown[...] = total

    for k in range(1, n_ctx):
        dst = lax.rem(me + n_ctx - k, n_ctx)
        send_if(me >= k, remote(sown, sin.at[me], s_s.at[k], s_r.at[me], ctx=dst))

    @pl.when(me < n_ctx - 1)
    def _():
        nxt = lax.rem(me + 1, n_ctx)
        remote(hsend, hrecv, h_s.at[0], h_r.at[0], ctx=nxt).wait_recv()
        remote(feat.at[pl.ds(1, 2), pl.ds(0, 16)], kvh, kv_s.at[0], kv_r.at[0], ctx=nxt).wait_recv()

    acts[0, pl.ds(length, 8)] = hrecv[pl.ds(0, 8)]

    def short(i):
        y = tv[i, pl.ds(0, 1)] * acts[i, pl.ds(0, length)]
        y = y + tv[i, pl.ds(1, 1)] * acts[i, pl.ds(1, length)]
        y = y + tv[i, pl.ds(2, 1)] * acts[i, pl.ds(2, length)]
        gp[i] = y.astype(BF16)

    short(0)

    ent[...] = jnp.zeros_like(ent)
    for j in range(n_ctx - 1, 0, -1):
        @pl.when(j > me)
        def _():
            remote(sown, sin.at[j], s_s.at[0], s_r.at[j], ctx=j).wait_recv()
            ent[...] = sin[j] + lam_ref[2] * ent[...]

    entering = ent[...]
    residue = rv[...]
    starts = [None] * CHAINS
    starts[CHAINS - 1] = entering
    for k in range(CHAINS - 2, -1, -1):
        starts[k] = csum[k + 1] + lam_ref[1] * starts[k + 1]

    def full_step(i, carry):
        states, totals = carry
        fresh, summed = [], []
        for k in range(CHAINS):
            r = k * run + run - 1 - i
            s = grow[pl.ds(r, 1)] + lam * states[k]
            gprod[pl.ds(r, 1)] = jnp.sum(residue * s, axis=0, keepdims=True)
            totals = totals + prod[pl.ds(r, 1)] * s
            fresh.append(s)
        return tuple(fresh), totals

    _, totals = lax.fori_loop(0, run, full_step, (tuple(starts), zero), unroll=4)
    rown[...] = totals
    beyond = (entering - hrecv[pl.ds(8, 1)]) * lam_ref[3]
    gprod[pl.ds(length, 1)] = jnp.sum(residue * entering, axis=0, keepdims=True)
    gprod[pl.ds(length + 1, 1)] = jnp.sum(residue * beyond, axis=0, keepdims=True)
    acts[1, pl.ds(0, length)] = gprod[pl.ds(0, length)] * fv[2].astype(F32)
    acts[2, pl.ds(0, length)] = gprod[pl.ds(0, length)] * fv[1].astype(F32)
    acts[1, pl.ds(length, 2)] = gprod[pl.ds(length, 2)] * kvh[1, pl.ds(0, 2)].astype(F32)
    acts[2, pl.ds(length, 2)] = gprod[pl.ds(length, 2)] * kvh[0, pl.ds(0, 2)].astype(F32)
    short(1)
    short(2)

    ready(7)

    def own_part(dest):
        at = pl.ds(pl.multiple_of(dest * length, length), length)
        y = lax.dot_general(iwv[0, at], gp[0], NT, preferred_element_type=F32)
        y = y + lax.dot_general(iwv[1, at], gp[1], NT, preferred_element_type=F32)
        y = y + lax.dot_general(iwv[2, at], gp[2], NT, preferred_element_type=F32)
        part[dest] = y

    def rs(item):
        i = INDEX[item]
        return remote(tx.at[i], rx.at[i], rs_s.at[i], rs_r.at[i], chan=back[LINK[item]])

    have = set()

    def summed(item):
        if item[:2] not in have:
            have.add(item[:2])
            own_part(place(item))
        y = part[place(item), rows(item[2])]
        for k in sorted(KIDS[item], key=lambda k: -START[k]):
            rs(k).wait_recv()
            y = y + rx[INDEX[k]].astype(F32)
        return y

    told = False
    for item in sorted(ITEMS, key=lambda item: (-HERE[item], -START[item])):
        if not told and END - HERE[item] > 4.0:
            told = True
            for k in range(1, n_ctx):
                dst = lax.rem(me + n_ctx - k, n_ctx)
                send(remote(rown, rin.at[me], r_s.at[k], r_r.at[me], ctx=dst))
        tx[INDEX[item]] = summed(item).astype(BF16)
        send(rs(item))
    for piece in range(PIECES):
        out[rows(piece)] = summed((0, 0, piece)).astype(BF16)

    rin[me] = rown[...]
    for k in range(1, n_ctx):
        src = lax.rem(me + k, n_ctx)
        remote(rown, rin.at[src], r_s.at[0], r_r.at[src], ctx=src).wait_recv()
    y = rin[0]
    for j in range(1, n_ctx):
        y = y + rin[j]
    gres[...] = y / (length * n_ctx)
    finish()


def local(features, saved_conv, grad_out, out_weight, in_weight, short_taps, residues, decay_time):
    length, width = grad_out.shape
    modes = residues.shape[0]
    n_chan = lax.axis_size("chan")
    n_ctx = lax.axis_size("ctx")
    dma = pltpu.SemaphoreType.DMA
    any_spec = pl.BlockSpec(memory_space=pl.ANY)
    vmem = pl.BlockSpec(memory_space=pltpu.VMEM)
    scratch = [
        pltpu.VMEM((n_chan, length, width), BF16),
        pltpu.VMEM(out_weight.shape, BF16),
        pltpu.VMEM(in_weight.shape, BF16),
        pltpu.VMEM(features.shape, BF16),
        pltpu.VMEM((length, width), BF16),
        pltpu.VMEM(short_taps.shape, F32),
        pltpu.VMEM((modes, width), F32),
        pltpu.VMEM((modes, width), F32),
        pltpu.VMEM((length, width), F32),
        pltpu.VMEM((length, width), F32),
        pltpu.VMEM((length, width), F32),
        pltpu.VMEM((3, length + 8, width), F32),
        pltpu.VMEM((3, length, width), BF16),
        pltpu.VMEM((length + 8, width), F32),
        pltpu.VMEM((4, modes, width), F32),
        pltpu.VMEM((modes, width), F32),
        pltpu.VMEM((CHAINS, modes, width), F32),
        pltpu.VMEM((modes, width), F32),
        pltpu.VMEM((n_ctx, modes, width), F32),
        pltpu.VMEM((16, width), F32),
        pltpu.VMEM((16, width), F32),
        pltpu.VMEM((2, 16, width), BF16),
        pltpu.VMEM((modes, width), F32),
        pltpu.VMEM((n_ctx, modes, width), F32),
        pltpu.VMEM((n_chan, length, width), F32),
        pltpu.VMEM((len(ITEMS), length // PIECES, width), BF16),
        pltpu.VMEM((len(ITEMS), length // PIECES, width), BF16),
        dma((8,)), dma((len(ITEMS),)), dma((len(ITEMS),)),
        dma((1,)), dma((1,)), dma((1,)), dma((1,)),
        dma((n_ctx,)), dma((n_ctx,)), dma((n_ctx,)), dma((n_ctx,)),
        dma((len(ITEMS),)), dma((len(ITEMS),)),
    ]
    return pl.pallas_call(
        kernel,
        out_shape=(
            jax.ShapeDtypeStruct((length, width), BF16),
            jax.ShapeDtypeStruct((modes, width), F32),
        ),
        in_specs=[any_spec] * 8,
        out_specs=(vmem, vmem),
        scratch_shapes=scratch,
        compiler_params=pltpu.CompilerParams(
            collective_id=0, has_side_effects=True, vmem_limit_bytes=67043328
        ),
    )(grad_out, features, saved_conv, out_weight, in_weight, short_taps, residues, decay_time)


def solution(mesh):
    return jax.shard_map(
        local,
        mesh=mesh,
        in_specs=(
            P(None, "ctx", "chan"),
            P("ctx", "chan"),
            P("ctx", "chan"),
            P("chan", None),
            P(None, None, "chan"),
            P(None, None, "chan"),
            P(None, "chan"),
            P(None, "chan"),
        ),
        out_specs=(P("chan", "ctx"), P(None, "chan")),
        check_vma=False,
    )
```

```python
import functools

import jax
import jax.numpy as jnp
from jax import lax
from jax.experimental import pallas as pl
from jax.experimental.pallas import tpu as pltpu
from jax.sharding import PartitionSpec as P

MESH = pl.DeviceIdType.MESH
F32 = jnp.float32
BF16 = jnp.bfloat16
NT = (((1,), (1,)), ((), ()))
CHAINS = 4

PIECES = 4
WIRE, HOP_Z, HOP_Y, AHEAD = 3.08 / PIECES, 2.2, 3.5, 1.6
CROSS = {1: (0, 1), 2: (0, 1, 2), 3: (0, 1), 4: ()}
OFFSETS = (-3, -2, -1, 0, 1, 2, 3, 4)


def origin(item, link):
    plane, off, piece = item
    if link == "y":
        return (0, off, piece)
    if link == "+":
        return (plane, (off if off < 4 else -4) + 1, piece)
    return (plane, off - 1, piece)


def schedule():
    link = {}
    for plane in (0, 1):
        for off in OFFSETS:
            for piece in range(PIECES):
                if off == 0:
                    how = "y" if plane else "own"
                elif plane and piece in CROSS[abs(off)]:
                    how = "y"
                elif off == 4:
                    how = "+" if piece < PIECES // 2 else "-"
                else:
                    how = "+" if off < 0 else "-"
                link[plane, off, piece] = how
    kids = {item: [] for item in link}
    for item, how in link.items():
        if how != "own":
            kids[origin(item, how)].append(item)

    def hop(item):
        return HOP_Y if link[item] == "y" else HOP_Z

    def height(item):
        return max([WIRE + hop(k) + height(k) for k in kids[item]], default=0.0)

    free = {"+": 0.0, "-": 0.0, "y": 0.0}
    queue = {"+": [], "-": [], "y": []}
    pending = [(0.0, p, (0, 0, p)) for p in range(PIECES)]
    here, start, now, count = {}, {}, 0.0, PIECES
    while True:
        times = [p[0] for p in pending] + [max(free[c], now) for c in queue if queue[c]]
        if not times:
            break
        now = min(times)
        for entry in sorted(p for p in pending if p[0] <= now + 1e-9):
            pending.remove(entry)
            here[entry[2]] = entry[0]
            for k in kids[entry[2]]:
                queue[link[k]].append((-height(k), now, k))
        for c in queue:
            if queue[c] and free[c] <= now + 1e-9:
                queue[c].sort()
                k = queue[c].pop(0)[2]
                start[k], free[c] = now, now + WIRE
                pending.append((now + WIRE + hop(k), count, k))
                count += 1
    return link, kids, here, start


LINK, KIDS, HERE, START = schedule()
ITEMS = sorted(START)
INDEX = {item: i for i, item in enumerate(ITEMS)}
END = max(HERE.values())
HALFWAY = sorted(ITEMS, key=lambda item: HERE[item])[len(ITEMS) // 2]


def kernel(
    go, feat, conv, ow, iw, taps, res, decay,
    out, gres,
    blocks, owv, iwv, fv, cv, tv, rv, dv,
    acc, grow, prod, acts, gp, gprod, lam_ref, ent, csum,
    sown, sin, hsend, hrecv, kvh, rown, rin,
    part, tx, rx,
    in_sem, ag_s, ag_r, kv_s, kv_r, h_s, h_r,
    s_s, s_r, r_s, r_r, rs_s, rs_r,
):
    n_ctx = lax.axis_size("ctx")
    n_z = lax.axis_size("chan") // 2
    me = lax.axis_index("ctx")
    ch = lax.axis_index("chan")
    z = ch // 2
    yh = lax.rem(ch, 2)
    length = acc.shape[0]

    def chan_of(zz, yy):
        return lax.rem(zz + 2 * n_z, n_z) * 2 + yy

    partner = chan_of(z, 1 - yh)
    sides = [chan_of(z + 1, yh), chan_of(z - 1, yh)]

    pairs = [(go, blocks.at[ch]), (ow, owv), (feat, fv), (conv, cv), (taps, tv),
             (res, rv), (decay, dv), (iw, iwv)]
    local = [pltpu.make_async_copy(a, b, in_sem.at[i]) for i, (a, b) in enumerate(pairs)]
    local[0].start()
    seen = set()

    def ready(*which):
        for i in which:
            if i not in seen:
                local[i].wait()
                seen.add(i)
    seen = set()

    def ready(*which):
        for i in which:
            if i not in seen:
                local[i].wait()
                seen.add(i)

    barrier = pltpu.get_barrier_semaphore()
    for dst in (sides[0], sides[1], partner):
        pl.semaphore_signal(barrier, inc=1, device_id={"chan": dst}, device_id_type=MESH)
    for k in range(1, n_ctx):
        pl.semaphore_signal(
            barrier, inc=1, device_id={"ctx": lax.rem(me + k, n_ctx)}, device_id_type=MESH
        )
    ready(0)
    pl.semaphore_wait(barrier, 3 + n_ctx - 1)

    def remote(src, dst, ss, rs, **where):
        return pltpu.make_async_remote_copy(
            src_ref=src, dst_ref=dst, send_sem=ss, recv_sem=rs,
            device_id=where, device_id_type=MESH,
        )

    piece_rows = length // PIECES

    def rows(piece):
        return pl.ds(piece * piece_rows, piece_rows)

    def place(item):
        return chan_of(z + item[1], yh if item[0] == 0 else 1 - yh)

    onward = {"+": sides[0], "-": sides[1], "y": partner}
    back = {"+": sides[1], "-": sides[0], "y": partner}

    def ag(item, receiving=False):
        held = item if receiving else origin(item, LINK[item])
        ref = blocks.at[place(held), rows(item[2])]
        i = INDEX[item]
        return remote(ref, ref, ag_s.at[i], ag_r.at[i], chan=onward[LINK[item]])

    sent = []
    guarded = []

    def finish():
        for c in sent:
            c.wait_send()
        for cond, c in guarded:
            pl.when(cond)(c.wait_send)

    def send_if(cond, c):
        pl.when(cond)(c.start)
        guarded.append((cond, c))

    def send(c):
        c.start()
        sent.append(c)

    steps = []
    for item in ITEMS:
        steps.append((max(HERE[origin(item, LINK[item])], START[item] - AHEAD), 1, item))
        steps.append((HERE[item], 0, item))
    steps.sort(key=lambda step: (step[0], step[1], START[step[2]]))
    head = [step for step in steps if step[1] == 1 and step[0] == 0.0]
    for _, _, item in head:
        send(ag(item))
    for c in local[1:7]:
        c.start()

    prev = lax.rem(me + n_ctx - 1, n_ctx)

    send_if(me > 0, remote(feat.at[pl.ds(1, 2), pl.ds(0, 16)], kvh, kv_s.at[0], kv_r.at[0], ctx=prev))

    @pl.when(me == n_ctx - 1)
    def _():
        kvh[...] = jnp.zeros_like(kvh)
        hrecv[...] = jnp.zeros_like(hrecv)

    first = [True]

    def multiply(block):
        cols = pl.ds(pl.multiple_of(block * length, length), length)
        term = lax.dot_general(blocks[block], owv[:, cols], NT, preferred_element_type=F32)
        if first[0]:
            acc[...] = term
            first[0] = False
        else:
            acc[...] += term

    ready(0, 1)
    multiply(ch)
    waiting = []
    arrived = {}
    prepared = False
    for when, kind, item in steps[len(head):]:
        if kind == 1:
            send(ag(item))
            continue
        ag(item, True).wait_recv()
        if item == HALFWAY:
            local[7].start()
        arrived[item[:2]] = arrived.get(item[:2], 0) + 1
        if waiting:
            multiply(place(waiting.pop(0) + (0,)))
        if arrived[item[:2]] == PIECES:
            waiting.append(item[:2])
        if not prepared and len(arrived) > 2:
            prepared = True
            ready(2, 3, 4, 5, 6)
            rate = 1.0 / dv[...]
            lam_ref[0] = jnp.exp(-rate)
            lam_ref[1] = jnp.exp(-rate * (length // CHAINS))
            lam_ref[2] = jnp.exp(-rate * length)
            lam_ref[3] = jnp.exp(rate)
            prod[...] = fv[1].astype(F32) * fv[2].astype(F32)
    for block in waiting:
        multiply(place(block + (0,)))

    gate = acc[...]
    grow[...] = gate * fv[0].astype(F32)
    acts[0, pl.ds(0, length)] = gate * cv[...].astype(F32)

    @pl.when(me > 0)
    def _():
        hsend[pl.ds(0, 8)] = acts[0, pl.ds(0, 8)]
        hsend[pl.ds(8, 8)] = grow[pl.ds(0, 8)]

    send_if(me > 0, remote(hsend, hrecv, h_s.at[0], h_r.at[0], ctx=prev))

    run = length // CHAINS
    lam = lam_ref[0]

    def sum_step(i, carry):
        fresh = []
        for k in range(CHAINS):
            g = grow[pl.ds(k * run + run - 1 - i, 1)]
            fresh.append(g + lam * carry[k])
        return tuple(fresh)

    zero = jnp.zeros_like(lam)
    sums = lax.fori_loop(0, run, sum_step, (zero,) * CHAINS, unroll=8)
    total = sums[CHAINS - 1]
    for k in range(CHAINS - 2, -1, -1):
        total = sums[k] + lam_ref[1] * total
    for k in range(CHAINS):
        csum[k] = sums[k]
    sown[...] = total

    for k in range(1, n_ctx):
        dst = lax.rem(me + n_ctx - k, n_ctx)
        send_if(me >= k, remote(sown, sin.at[me], s_s.at[k], s_r.at[me], ctx=dst))

    @pl.when(me < n_ctx - 1)
    def _():
        nxt = lax.rem(me + 1, n_ctx)
        remote(hsend, hrecv, h_s.at[0], h_r.at[0], ctx=nxt).wait_recv()
        remote(feat.at[pl.ds(1, 2), pl.ds(0, 16)], kvh, kv_s.at[0], kv_r.at[0], ctx=nxt).wait_recv()

    acts[0, pl.ds(length, 8)] = hrecv[pl.ds(0, 8)]

    def short(i):
        y = tv[i, pl.ds(0, 1)] * acts[i, pl.ds(0, length)]
        y = y + tv[i, pl.ds(1, 1)] * acts[i, pl.ds(1, length)]
        y = y + tv[i, pl.ds(2, 1)] * acts[i, pl.ds(2, length)]
        gp[i] = y.astype(BF16)

    short(0)

    ent[...] = jnp.zeros_like(ent)
    for j in range(n_ctx - 1, 0, -1):
        @pl.when(j > me)
        def _():
            remote(sown, sin.at[j], s_s.at[0], s_r.at[j], ctx=j).wait_recv()
            ent[...] = sin[j] + lam_ref[2] * ent[...]

    entering = ent[...]
    residue = rv[...]
    starts = [None] * CHAINS
    starts[CHAINS - 1] = entering
    for k in range(CHAINS - 2, -1, -1):
        starts[k] = csum[k + 1] + lam_ref[1] * starts[k + 1]

    def full_step(i, carry):
        states, totals = carry
        fresh, summed = [], []
        for k in range(CHAINS):
            r = k * run + run - 1 - i
            s = grow[pl.ds(r, 1)] + lam * states[k]
            gprod[pl.ds(r, 1)] = jnp.sum(residue * s, axis=0, keepdims=True)
            totals = totals + prod[pl.ds(r, 1)] * s
            fresh.append(s)
        return tuple(fresh), totals

    _, totals = lax.fori_loop(0, run, full_step, (tuple(starts), zero), unroll=4)
    rown[...] = totals
    beyond = (entering - hrecv[pl.ds(8, 1)]) * lam_ref[3]
    gprod[pl.ds(length, 1)] = jnp.sum(residue * entering, axis=0, keepdims=True)
    gprod[pl.ds(length + 1, 1)] = jnp.sum(residue * beyond, axis=0, keepdims=True)
    acts[1, pl.ds(0, length)] = gprod[pl.ds(0, length)] * fv[2].astype(F32)
    acts[2, pl.ds(0, length)] = gprod[pl.ds(0, length)] * fv[1].astype(F32)
    acts[1, pl.ds(length, 2)] = gprod[pl.ds(length, 2)] * kvh[1, pl.ds(0, 2)].astype(F32)
    acts[2, pl.ds(length, 2)] = gprod[pl.ds(length, 2)] * kvh[0, pl.ds(0, 2)].astype(F32)
    short(1)
    short(2)

    ready(7)

    def own_part(dest):
        at = pl.ds(pl.multiple_of(dest * length, length), length)
        y = lax.dot_general(iwv[0, at], gp[0], NT, preferred_element_type=F32)
        y = y + lax.dot_general(iwv[1, at], gp[1], NT, preferred_element_type=F32)
        y = y + lax.dot_general(iwv[2, at], gp[2], NT, preferred_element_type=F32)
        part[dest] = y

    def rs(item):
        i = INDEX[item]
        return remote(tx.at[i], rx.at[i], rs_s.at[i], rs_r.at[i], chan=back[LINK[item]])

    have = set()

    def summed(item):
        if item[:2] not in have:
            have.add(item[:2])
            own_part(place(item))
        y = part[place(item), rows(item[2])]
        for k in sorted(KIDS[item], key=lambda k: -START[k]):
            rs(k).wait_recv()
            y = y + rx[INDEX[k]].astype(F32)
        return y

    told = False
    for item in sorted(ITEMS, key=lambda item: (-HERE[item], -START[item])):
        if not told and END - HERE[item] > 4.0:
            told = True
            for k in range(1, n_ctx):
                dst = lax.rem(me + n_ctx - k, n_ctx)
                send(remote(rown, rin.at[me], r_s.at[k], r_r.at[me], ctx=dst))
        tx[INDEX[item]] = summed(item).astype(BF16)
        send(rs(item))
    for piece in range(PIECES):
        out[rows(piece)] = summed((0, 0, piece)).astype(BF16)

    rin[me] = rown[...]
    for k in range(1, n_ctx):
        src = lax.rem(me + k, n_ctx)
        remote(rown, rin.at[src], r_s.at[0], r_r.at[src], ctx=src).wait_recv()
    y = rin[0]
    for j in range(1, n_ctx):
        y = y + rin[j]
    gres[...] = y / (length * n_ctx)
    finish()


def local(features, saved_conv, grad_out, out_weight, in_weight, short_taps, residues, decay_time):
    length, width = grad_out.shape
    modes = residues.shape[0]
    n_chan = lax.axis_size("chan")
    n_ctx = lax.axis_size("ctx")
    dma = pltpu.SemaphoreType.DMA
    any_spec = pl.BlockSpec(memory_space=pl.ANY)
    vmem = pl.BlockSpec(memory_space=pltpu.VMEM)
    scratch = [
        pltpu.VMEM((n_chan, length, width), BF16),
        pltpu.VMEM(out_weight.shape, BF16),
        pltpu.VMEM(in_weight.shape, BF16),
        pltpu.VMEM(features.shape, BF16),
        pltpu.VMEM((length, width), BF16),
        pltpu.VMEM(short_taps.shape, F32),
        pltpu.VMEM((modes, width), F32),
        pltpu.VMEM((modes, width), F32),
        pltpu.VMEM((length, width), F32),
        pltpu.VMEM((length, width), F32),
        pltpu.VMEM((length, width), F32),
        pltpu.VMEM((3, length + 8, width), F32),
        pltpu.VMEM((3, length, width), BF16),
        pltpu.VMEM((length + 8, width), F32),
        pltpu.VMEM((4, modes, width), F32),
        pltpu.VMEM((modes, width), F32),
        pltpu.VMEM((CHAINS, modes, width), F32),
        pltpu.VMEM((modes, width), F32),
        pltpu.VMEM((n_ctx, modes, width), F32),
        pltpu.VMEM((16, width), F32),
        pltpu.VMEM((16, width), F32),
        pltpu.VMEM((2, 16, width), BF16),
        pltpu.VMEM((modes, width), F32),
        pltpu.VMEM((n_ctx, modes, width), F32),
        pltpu.VMEM((n_chan, length, width), F32),
        pltpu.VMEM((len(ITEMS), length // PIECES, width), BF16),
        pltpu.VMEM((len(ITEMS), length // PIECES, width), BF16),
        dma((8,)), dma((len(ITEMS),)), dma((len(ITEMS),)),
        dma((1,)), dma((1,)), dma((1,)), dma((1,)),
        dma((n_ctx,)), dma((n_ctx,)), dma((n_ctx,)), dma((n_ctx,)),
        dma((len(ITEMS),)), dma((len(ITEMS),)),
    ]
    return pl.pallas_call(
        kernel,
        out_shape=(
            jax.ShapeDtypeStruct((length, width), BF16),
            jax.ShapeDtypeStruct((modes, width), F32),
        ),
        in_specs=[any_spec] * 8,
        out_specs=(vmem, vmem),
        scratch_shapes=scratch,
        compiler_params=pltpu.CompilerParams(
            collective_id=0, has_side_effects=True, vmem_limit_bytes=67043328
        ),
    )(grad_out, features, saved_conv, out_weight, in_weight, short_taps, residues, decay_time)


def solution(mesh):
    return jax.shard_map(
        local,
        mesh=mesh,
        in_specs=(
            P(None, "ctx", "chan"),
            P("ctx", "chan"),
            P("ctx", "chan"),
            P("chan", None),
            P(None, None, "chan"),
            P(None, None, "chan"),
            P(None, "chan"),
            P(None, "chan"),
        ),
        out_specs=(P("chan", "ctx"), P(None, "chan")),
        check_vma=False,
    )
```

```python
import functools

import jax
import jax.numpy as jnp
from jax import lax
from jax.experimental import pallas as pl
from jax.experimental.pallas import tpu as pltpu
from jax.sharding import PartitionSpec as P

MESH = pl.DeviceIdType.MESH
F32 = jnp.float32
BF16 = jnp.bfloat16
NT = (((1,), (1,)), ((), ()))
CHAINS = 4

PIECES = 4
WIRE, HOP_Z, HOP_Y, AHEAD = 3.08 / PIECES, 2.2, 3.5, 1.6
CROSS = {1: (0, 1), 2: (0, 1, 2), 3: (0, 1), 4: ()}
OFFSETS = (-3, -2, -1, 0, 1, 2, 3, 4)


def origin(item, link):
    plane, off, piece = item
    if link == "y":
        return (0, off, piece)
    if link == "+":
        return (plane, (off if off < 4 else -4) + 1, piece)
    return (plane, off - 1, piece)


def schedule():
    link = {}
    for plane in (0, 1):
        for off in OFFSETS:
            for piece in range(PIECES):
                if off == 0:
                    how = "y" if plane else "own"
                elif plane and piece in CROSS[abs(off)]:
                    how = "y"
                elif off == 4:
                    how = "+" if piece < PIECES // 2 else "-"
                else:
                    how = "+" if off < 0 else "-"
                link[plane, off, piece] = how
    kids = {item: [] for item in link}
    for item, how in link.items():
        if how != "own":
            kids[origin(item, how)].append(item)

    def hop(item):
        return HOP_Y if link[item] == "y" else HOP_Z

    def height(item):
        return max([WIRE + hop(k) + height(k) for k in kids[item]], default=0.0)

    free = {"+": 0.0, "-": 0.0, "y": 0.0}
    queue = {"+": [], "-": [], "y": []}
    pending = [(0.0, p, (0, 0, p)) for p in range(PIECES)]
    here, start, now, count = {}, {}, 0.0, PIECES
    while True:
        times = [p[0] for p in pending] + [max(free[c], now) for c in queue if queue[c]]
        if not times:
            break
        now = min(times)
        for entry in sorted(p for p in pending if p[0] <= now + 1e-9):
            pending.remove(entry)
            here[entry[2]] = entry[0]
            for k in kids[entry[2]]:
                queue[link[k]].append((-height(k), now, k))
        for c in queue:
            if queue[c] and free[c] <= now + 1e-9:
                queue[c].sort()
                k = queue[c].pop(0)[2]
                start[k], free[c] = now, now + WIRE
                pending.append((now + WIRE + hop(k), count, k))
                count += 1
    return link, kids, here, start


LINK, KIDS, HERE, START = schedule()
ITEMS = sorted(START)
INDEX = {item: i for i, item in enumerate(ITEMS)}
END = max(HERE.values())
HALFWAY = sorted(ITEMS, key=lambda item: HERE[item])[len(ITEMS) // 2]


def kernel(
    go, feat, conv, ow, iw, taps, res, decay,
    out, gres,
    blocks, owv, iwv, fv, cv, tv, rv, dv,
    acc, grow, prod, acts, gp, gprod, lam_ref, ent, csum,
    sown, sin, hsend, hrecv, kvh, rown, rin,
    part, tx, rx,
    in_sem, ag_s, ag_r, kv_s, kv_r, h_s, h_r,
    s_s, s_r, r_s, r_r, rs_s, rs_r,
):
    n_ctx = lax.axis_size("ctx")
    n_z = lax.axis_size("chan") // 2
    me = lax.axis_index("ctx")
    ch = lax.axis_index("chan")
    z = ch // 2
    yh = lax.rem(ch, 2)
    length = acc.shape[0]

    def chan_of(zz, yy):
        return lax.rem(zz + 2 * n_z, n_z) * 2 + yy

    partner = chan_of(z, 1 - yh)
    sides = [chan_of(z + 1, yh), chan_of(z - 1, yh)]

    pairs = [(go, blocks.at[ch]), (ow, owv), (feat, fv), (conv, cv), (taps, tv),
             (res, rv), (decay, dv), (iw, iwv)]
    local = [pltpu.make_async_copy(a, b, in_sem.at[i]) for i, (a, b) in enumerate(pairs)]
    local[0].start()
    seen = set()

    def ready(*which):
        for i in which:
            if i not in seen:
                local[i].wait()
                seen.add(i)
    seen = set()

    def ready(*which):
        for i in which:
            if i not in seen:
                local[i].wait()
                seen.add(i)

    barrier = pltpu.get_barrier_semaphore()
    for dst in (sides[0], sides[1], partner):
        pl.semaphore_signal(barrier, inc=1, device_id={"chan": dst}, device_id_type=MESH)
    for k in range(1, n_ctx):
        pl.semaphore_signal(
            barrier, inc=1, device_id={"ctx": lax.rem(me + k, n_ctx)}, device_id_type=MESH
        )
    ready(0)
    pl.semaphore_wait(barrier, 3 + n_ctx - 1)

    def remote(src, dst, ss, rs, **where):
        return pltpu.make_async_remote_copy(
            src_ref=src, dst_ref=dst, send_sem=ss, recv_sem=rs,
            device_id=where, device_id_type=MESH,
        )

    piece_rows = length // PIECES

    def rows(piece):
        return pl.ds(piece * piece_rows, piece_rows)

    def place(item):
        return chan_of(z + item[1], yh if item[0] == 0 else 1 - yh)

    onward = {"+": sides[0], "-": sides[1], "y": partner}
    back = {"+": sides[1], "-": sides[0], "y": partner}

    def ag(item, receiving=False):
        held = item if receiving else origin(item, LINK[item])
        ref = blocks.at[place(held), rows(item[2])]
        i = INDEX[item]
        return remote(ref, ref, ag_s.at[i], ag_r.at[i], chan=onward[LINK[item]])

    sent = []
    guarded = []

    def finish():
        for c in sent:
            c.wait_send()
        for cond, c in guarded:
            pl.when(cond)(c.wait_send)

    def send_if(cond, c):
        pl.when(cond)(c.start)
        guarded.append((cond, c))

    def send(c):
        c.start()
        sent.append(c)

    steps = []
    for item in ITEMS:
        steps.append((max(HERE[origin(item, LINK[item])], START[item] - AHEAD), 1, item))
        steps.append((HERE[item], 0, item))
    steps.sort(key=lambda step: (step[0], step[1], START[step[2]]))
    head = [step for step in steps if step[1] == 1 and step[0] == 0.0]
    for _, _, item in head:
        send(ag(item))
    for c in local[1:7]:
        c.start()

    prev = lax.rem(me + n_ctx - 1, n_ctx)

    send_if(me > 0, remote(feat.at[pl.ds(1, 2), pl.ds(0, 16)], kvh, kv_s.at[0], kv_r.at[0], ctx=prev))

    @pl.when(me == n_ctx - 1)
    def _():
        kvh[...] = jnp.zeros_like(kvh)
        hrecv[...] = jnp.zeros_like(hrecv)

    first = [True]

    def multiply(block):
        cols = pl.ds(pl.multiple_of(block * length, length), length)
        term = lax.dot_general(blocks[block], owv[:, cols], NT, preferred_element_type=F32)
        if first[0]:
            acc[...] = term
            first[0] = False
        else:
            acc[...] += term

    ready(0, 1)
    multiply(ch)
    waiting = []
    arrived = {}
    prepared = False
    for when, kind, item in steps[len(head):]:
        if kind == 1:
            send(ag(item))
            continue
        ag(item, True).wait_recv()
        if item == HALFWAY:
            local[7].start()
        arrived[item[:2]] = arrived.get(item[:2], 0) + 1
        if waiting:
            multiply(place(waiting.pop(0) + (0,)))
        if arrived[item[:2]] == PIECES:
            waiting.append(item[:2])
        if not prepared and len(arrived) > 2:
            prepared = True
            ready(2, 3, 4, 5, 6)
            rate = 1.0 / dv[...]
            lam_ref[0] = jnp.exp(-rate)
            lam_ref[1] = jnp.exp(-rate * (length // CHAINS))
            lam_ref[2] = jnp.exp(-rate * length)
            lam_ref[3] = jnp.exp(rate)
            prod[...] = fv[1].astype(F32) * fv[2].astype(F32)
    for block in waiting:
        multiply(place(block + (0,)))

    gate = acc[...]
    grow[...] = gate * fv[0].astype(F32)
    acts[0, pl.ds(0, length)] = gate * cv[...].astype(F32)

    @pl.when(me > 0)
    def _():
        hsend[pl.ds(0, 8)] = acts[0, pl.ds(0, 8)]
        hsend[pl.ds(8, 8)] = grow[pl.ds(0, 8)]

    send_if(me > 0, remote(hsend, hrecv, h_s.at[0], h_r.at[0], ctx=prev))

    run = length // CHAINS
    lam = lam_ref[0]

    def sum_step(i, carry):
        fresh = []
        for k in range(CHAINS):
            g = grow[pl.ds(k * run + run - 1 - i, 1)]
            fresh.append(g + lam * carry[k])
        return tuple(fresh)

    zero = jnp.zeros_like(lam)
    sums = lax.fori_loop(0, run, sum_step, (zero,) * CHAINS, unroll=8)
    total = sums[CHAINS - 1]
    for k in range(CHAINS - 2, -1, -1):
        total = sums[k] + lam_ref[1] * total
    for k in range(CHAINS):
        csum[k] = sums[k]
    sown[...] = total.astype(BF16)

    for k in range(1, n_ctx):
        dst = lax.rem(me + n_ctx - k, n_ctx)
        send_if(me >= k, remote(sown, sin.at[me], s_s.at[k], s_r.at[me], ctx=dst))

    @pl.when(me < n_ctx - 1)
    def _():
        nxt = lax.rem(me + 1, n_ctx)
        remote(hsend, hrecv, h_s.at[0], h_r.at[0], ctx=nxt).wait_recv()
        remote(feat.at[pl.ds(1, 2), pl.ds(0, 16)], kvh, kv_s.at[0], kv_r.at[0], ctx=nxt).wait_recv()

    acts[0, pl.ds(length, 8)] = hrecv[pl.ds(0, 8)]

    def short(i):
        y = tv[i, pl.ds(0, 1)] * acts[i, pl.ds(0, length)]
        y = y + tv[i, pl.ds(1, 1)] * acts[i, pl.ds(1, length)]
        y = y + tv[i, pl.ds(2, 1)] * acts[i, pl.ds(2, length)]
        gp[i] = y.astype(BF16)

    short(0)

    ent[...] = jnp.zeros_like(ent)
    for j in range(n_ctx - 1, 0, -1):
        @pl.when(j > me)
        def _():
            remote(sown, sin.at[j], s_s.at[0], s_r.at[j], ctx=j).wait_recv()
            ent[...] = sin[j].astype(F32) + lam_ref[2] * ent[...]

    entering = ent[...]
    residue = rv[...]
    starts = [None] * CHAINS
    starts[CHAINS - 1] = entering
    for k in range(CHAINS - 2, -1, -1):
        starts[k] = csum[k + 1] + lam_ref[1] * starts[k + 1]

    def full_step(i, carry):
        states, totals = carry
        fresh, summed = [], []
        for k in range(CHAINS):
            r = k * run + run - 1 - i
            s = grow[pl.ds(r, 1)] + lam * states[k]
            gprod[pl.ds(r, 1)] = jnp.sum(residue * s, axis=0, keepdims=True)
            totals = totals + prod[pl.ds(r, 1)] * s
            fresh.append(s)
        return tuple(fresh), totals

    _, totals = lax.fori_loop(0, run, full_step, (tuple(starts), zero), unroll=4)
    rown[...] = totals
    beyond = (entering - hrecv[pl.ds(8, 1)]) * lam_ref[3]
    gprod[pl.ds(length, 1)] = jnp.sum(residue * entering, axis=0, keepdims=True)
    gprod[pl.ds(length + 1, 1)] = jnp.sum(residue * beyond, axis=0, keepdims=True)
    acts[1, pl.ds(0, length)] = gprod[pl.ds(0, length)] * fv[2].astype(F32)
    acts[2, pl.ds(0, length)] = gprod[pl.ds(0, length)] * fv[1].astype(F32)
    acts[1, pl.ds(length, 2)] = gprod[pl.ds(length, 2)] * kvh[1, pl.ds(0, 2)].astype(F32)
    acts[2, pl.ds(length, 2)] = gprod[pl.ds(length, 2)] * kvh[0, pl.ds(0, 2)].astype(F32)
    short(1)
    short(2)

    ready(7)

    def own_part(dest):
        at = pl.ds(pl.multiple_of(dest * length, length), length)
        y = lax.dot_general(iwv[0, at], gp[0], NT, preferred_element_type=F32)
        y = y + lax.dot_general(iwv[1, at], gp[1], NT, preferred_element_type=F32)
        y = y + lax.dot_general(iwv[2, at], gp[2], NT, preferred_element_type=F32)
        part[dest] = y

    def rs(item):
        i = INDEX[item]
        return remote(tx.at[i], rx.at[i], rs_s.at[i], rs_r.at[i], chan=back[LINK[item]])

    have = set()

    def summed(item):
        if item[:2] not in have:
            have.add(item[:2])
            own_part(place(item))
        y = part[place(item), rows(item[2])]
        for k in sorted(KIDS[item], key=lambda k: -START[k]):
            rs(k).wait_recv()
            y = y + rx[INDEX[k]].astype(F32)
        return y

    told = False
    for item in sorted(ITEMS, key=lambda item: (-HERE[item], -START[item])):
        if not told and END - HERE[item] > 4.0:
            told = True
            for k in range(1, n_ctx):
                dst = lax.rem(me + n_ctx - k, n_ctx)
                send(remote(rown, rin.at[me], r_s.at[k], r_r.at[me], ctx=dst))
        tx[INDEX[item]] = summed(item).astype(BF16)
        send(rs(item))
    for piece in range(PIECES):
        out[rows(piece)] = summed((0, 0, piece)).astype(BF16)

    rin[me] = rown[...]
    for k in range(1, n_ctx):
        src = lax.rem(me + k, n_ctx)
        remote(rown, rin.at[src], r_s.at[0], r_r.at[src], ctx=src).wait_recv()
    y = rin[0]
    for j in range(1, n_ctx):
        y = y + rin[j]
    gres[...] = y / (length * n_ctx)
    finish()


def local(features, saved_conv, grad_out, out_weight, in_weight, short_taps, residues, decay_time):
    length, width = grad_out.shape
    modes = residues.shape[0]
    n_chan = lax.axis_size("chan")
    n_ctx = lax.axis_size("ctx")
    dma = pltpu.SemaphoreType.DMA
    any_spec = pl.BlockSpec(memory_space=pl.ANY)
    vmem = pl.BlockSpec(memory_space=pltpu.VMEM)
    scratch = [
        pltpu.VMEM((n_chan, length, width), BF16),
        pltpu.VMEM(out_weight.shape, BF16),
        pltpu.VMEM(in_weight.shape, BF16),
        pltpu.VMEM(features.shape, BF16),
        pltpu.VMEM((length, width), BF16),
        pltpu.VMEM(short_taps.shape, F32),
        pltpu.VMEM((modes, width), F32),
        pltpu.VMEM((modes, width), F32),
        pltpu.VMEM((length, width), F32),
        pltpu.VMEM((length, width), F32),
        pltpu.VMEM((length, width), F32),
        pltpu.VMEM((3, length + 8, width), F32),
        pltpu.VMEM((3, length, width), BF16),
        pltpu.VMEM((length + 8, width), F32),
        pltpu.VMEM((4, modes, width), F32),
        pltpu.VMEM((modes, width), F32),
        pltpu.VMEM((CHAINS, modes, width), F32),
        pltpu.VMEM((modes, width), BF16),
        pltpu.VMEM((n_ctx, modes, width), BF16),
        pltpu.VMEM((16, width), F32),
        pltpu.VMEM((16, width), F32),
        pltpu.VMEM((2, 16, width), BF16),
        pltpu.VMEM((modes, width), F32),
        pltpu.VMEM((n_ctx, modes, width), F32),
        pltpu.VMEM((n_chan, length, width), F32),
        pltpu.VMEM((len(ITEMS), length // PIECES, width), BF16),
        pltpu.VMEM((len(ITEMS), length // PIECES, width), BF16),
        dma((8,)), dma((len(ITEMS),)), dma((len(ITEMS),)),
        dma((1,)), dma((1,)), dma((1,)), dma((1,)),
        dma((n_ctx,)), dma((n_ctx,)), dma((n_ctx,)), dma((n_ctx,)),
        dma((len(ITEMS),)), dma((len(ITEMS),)),
    ]
    return pl.pallas_call(
        kernel,
        out_shape=(
            jax.ShapeDtypeStruct((length, width), BF16),
            jax.ShapeDtypeStruct((modes, width), F32),
        ),
        in_specs=[any_spec] * 8,
        out_specs=(vmem, vmem),
        scratch_shapes=scratch,
        compiler_params=pltpu.CompilerParams(
            collective_id=0, has_side_effects=True, vmem_limit_bytes=67043328
        ),
    )(grad_out, features, saved_conv, out_weight, in_weight, short_taps, residues, decay_time)


def solution(mesh):
    return jax.shard_map(
        local,
        mesh=mesh,
        in_specs=(
            P(None, "ctx", "chan"),
            P("ctx", "chan"),
            P("ctx", "chan"),
            P("chan", None),
            P(None, None, "chan"),
            P(None, None, "chan"),
            P(None, "chan"),
            P(None, "chan"),
        ),
        out_specs=(P("chan", "ctx"), P(None, "chan")),
        check_vma=False,
    )
```
